32 devices in a mesh: wide: 8 (over y, x, core), narrow: 4 (over z).
Axes of the slice: x: 2, y: 2, z: 4, core: 2. Of those that a mesh axis runs over, the one named last changes fastest.
Arguments:
- tokens: bfloat16 [16384, 768], P(('wide', 'narrow')), may hold values from -6 to 6
- cotangent: bfloat16 [16384, 768], P(('wide', 'narrow')), may hold values from -6 to 6
- passage_lengths: int32 [32, 8], P(('wide', 'narrow')), may hold values from 1 to 384, as said below
- passage_counts: int32 [32], P(('wide', 'narrow')), may hold values from 2 to 8
- pad_counts: int32 [32], P(('wide', 'narrow')), may hold values from 0 to 64, as said below
- w_qkv: bfloat16 [768, 2304], P(('wide', 'narrow')), may hold values from -0.21875 to 0.21875
- b_query: bfloat16 [768], P(('wide', 'narrow')), may hold values from -3 to 3
- b_value: bfloat16 [768], P(('wide', 'narrow')), may hold values from -3 to 3
- w_out: bfloat16 [768, 768], P(('wide', 'narrow')), may hold values from -0.625 to 0.625
- b_out: bfloat16 [768], P(('wide', 'narrow')), may hold values from -3 to 3
- ln1_gain: bfloat16 [768], P(('wide', 'narrow')), may hold values from 0.5 to 1.5
- ln1_bias: bfloat16 [768], P(('wide', 'narrow')), may hold values from -3 to 3
- w_in: bfloat16 [768, 3072], P(('wide', 'narrow')), may hold values from -0.21875 to 0.21875
- b_in: bfloat16 [3072], P(('wide', 'narrow')), may hold values from -3 to 3
- w_down: bfloat16 [3072, 768], P(('wide', 'narrow')), may hold values from -0.109375 to 0.109375
- b_down: bfloat16 [768], P(('wide', 'narrow')), may hold values from -3 to 3
- ln2_gain: bfloat16 [768], P(('wide', 'narrow')), may hold values from 0.5 to 1.5
- ln2_bias: bfloat16 [768], P(('wide', 'narrow')), may hold values from -3 to 3
Outputs:
- activations: bfloat16 [16384, 768], P(('wide', 'narrow'))
- token_grad: bfloat16 [16384, 768], P(('wide', 'narrow'))
- w_qkv_grad: float32 [768, 2304], P(('wide', 'narrow'))
- b_query_grad: float32 [768], P(('wide', 'narrow'))
- b_value_grad: float32 [768], P(('wide', 'narrow'))
- w_out_grad: float32 [768, 768], P(('wide', 'narrow'))
- b_out_grad: float32 [768], P(('wide', 'narrow'))
- ln1_gain_grad: float32 [768], P(('wide', 'narrow'))
- ln1_bias_grad: float32 [768], P(('wide', 'narrow'))
- w_in_grad: float32 [768, 3072], P(('wide', 'narrow'))
- b_in_grad: float32 [3072], P(('wide', 'narrow'))
- w_down_grad: float32 [3072, 768], P(('wide', 'narrow'))
- b_down_grad: float32 [768], P(('wide', 'narrow'))
- ln2_gain_grad: float32 [768], P(('wide', 'narrow'))
- ln2_bias_grad: float32 [768], P(('wide', 'narrow'))
The draws below stay inside these ranges and needn't reach their ends.
Inputs may be any that keep to these rules, and one draw needn't show every extreme that they name: passage j of row r, for j < passage_counts[r] - 1, has passage_lengths[r, j] positions; passages follow each other from position 0, the last one runs up to the padding; entries from j = passage_counts[r] - 1 on are not needed. The padding is the last pad_counts[r] positions of row r.
All inputs are finite; a program needn't handle non-finite values.
Results may differ from the reference program's by a relative error of at most 0.014.
Values may be sent and summed in bfloat16 or wider, within the bound.
A program may use at most 192 MiB of HBM per device.

```python
import math
import jax
import jax.numpy as jnp
from jax import lax

D = 768
HD = 64
FF = 3072
SEQ_LEN = 512
MAXP = 8
PADMAX = 64
SEQS = 32
TOKENS = 16384


def draw_layout(key):
    base_key = jax.random.fold_in(key, 7)
    key_count, key_pad, key_rows, key_shift, key_fill = jax.random.split(base_key, 5)
    counts = jax.random.randint(key_count, (SEQS,), 2, MAXP + 1).astype(jnp.int32)
    pads = jax.random.randint(key_pad, (SEQS,), 0, PADMAX + 1).astype(jnp.int32)
    chosen = jax.random.permutation(key_rows, SEQS)[:4]
    counts = counts.at[chosen[0]].set(MAXP).at[chosen[1]].set(2)
    pads = pads.at[chosen[2]].set(PADMAX).at[chosen[3]].set(0).at[chosen[1]].set(0)
    live = SEQ_LEN - pads
    base = live // counts
    extra = live - base * counts
    slots = jnp.arange(MAXP, dtype=jnp.int32)
    lengths = base[:, None] + (slots[None, :] < extra[:, None]).astype(jnp.int32)
    half = base // 2
    shifts = jax.random.randint(key_shift, (SEQS, MAXP // 2), 0, 1 << 20).astype(jnp.int32) % (2 * half[:, None] + 1) - half[:, None]
    shifts = shifts.at[chosen[1], 0].set(half[chosen[1]])
    paired = slots[1::2][None, :] < counts[:, None]
    shifts = jnp.where(paired, shifts, 0)
    signs = jnp.tile(jnp.array([1, -1], dtype=jnp.int32), MAXP // 2)
    lengths = lengths + jnp.repeat(shifts, 2, axis=1) * signs[None, :]
    filler = 1 + jax.random.randint(key_fill, (SEQS, MAXP), 0, 1 << 20).astype(jnp.int32) % base[:, None]
    lengths = jnp.where(slots[None, :] < counts[:, None], lengths, filler)
    return (lengths.astype(jnp.int32), counts, pads)


def draw_passage_lengths(key, part):
    return draw_layout(key)[0]


def draw_passage_counts(key, part):
    return draw_layout(key)[1]


def draw_pad_counts(key, part):
    return draw_layout(key)[2]


def raised(values, own_key, source, target, shards_of, factor):
    owner, partner = [(jnp.arange(values.shape[dim]) // (values.shape[dim] // shards_of)).reshape([-1 if axis == dim else 1 for axis in range(values.ndim)]) for dim in (source, target)]
    chosen = jax.random.permutation(own_key, shards_of)[partner]
    strong = (owner == chosen) | (owner == (partner + shards_of // 2) % shards_of)
    return jnp.where(strong, factor * values, values)


def shard_levels(own_key, shape, shards, smallest, largest):
    def one(axis_at, parts):
        steps = jax.random.uniform(jax.random.fold_in(jax.random.fold_in(own_key, 6), axis_at), (parts,), jnp.float32, smallest / len(shards), largest / len(shards))
        return jnp.repeat(jnp.exp(steps), shape[axis_at] // parts).reshape((-1,) + (1,) * (len(shape) - axis_at - 1))

    level = one(*shards[0])
    for cut in shards[1:]:
        level = level * one(*cut)
    return level


def noise(stream_key, dims, spread, reach, shards=(), held_as=jnp.bfloat16):
    level = shard_levels(stream_key, dims, shards, -0.22, 0.18) if shards else 1.0
    entries = jax.random.normal(stream_key, dims, jnp.float32) * spread * level
    return jnp.minimum(jnp.maximum(entries, -reach), reach).astype(held_as)


def bell_draw_with(stream_key, extent, scale, limit, shards, heavy, held_as=jnp.bfloat16):
    values = scale * jax.random.normal(stream_key, extent, jnp.float32)
    if shards:
        values = values * shard_levels(stream_key, extent, shards, -0.22, 0.18)
    return jnp.clip(raised(values, jax.random.fold_in(stream_key, 3), *heavy), -limit, limit).astype(held_as)


def setup_inputs(seed: int = 0) -> dict:
    splits = jax.random.split(jax.random.key(seed), 19)
    tokens = noise(splits[0], (TOKENS, D), 1.0, 6.0, ((0, 32),))
    cotangent = bell_draw_with(splits[1], (TOKENS, D), 1.0, 6.0, ((0, 32),), (0, 1, 32, 2.75))
    passage_lengths = draw_passage_lengths(jax.random.fold_in(splits[18], 71), 0)
    passage_counts = draw_passage_counts(jax.random.fold_in(splits[18], 71), 0)
    pad_counts = draw_pad_counts(jax.random.fold_in(splits[18], 71), 0)
    w_qkv = noise(splits[5], (D, 3 * D), D ** -0.5, 0.21875, ((0, 32),))
    b_query = noise(splits[6], (D,), 0.5, 3.0, ((0, 32),))
    b_value = noise(splits[7], (D,), 0.5, 3.0, ((0, 32),))
    w_out = noise(splits[8], (D, D), (D // 8) ** -0.5, 0.625, ((0, 32),))
    b_out = noise(splits[9], (D,), 0.5, 3.0, ((0, 32),))
    ln1_gain = jnp.clip(1.0 + 0.1 * jax.random.normal(splits[10], (D,), jnp.float32), 0.5, 1.5).astype(jnp.bfloat16)
    ln1_bias = noise(splits[11], (D,), 0.5, 3.0, ((0, 32),))
    w_in = noise(splits[12], (D, FF), D ** -0.5, 0.21875, ((0, 32),))
    b_in = noise(splits[13], (FF,), 0.5, 3.0, ((0, 32),))
    w_down = noise(splits[14], (FF, D), FF ** -0.5, 0.109375, ((0, 32),))
    b_down = noise(splits[15], (D,), 0.5, 3.0, ((0, 32),))
    ln2_gain = jnp.clip(1.0 + 0.1 * jax.random.normal(splits[16], (D,), jnp.float32), 0.5, 1.5).astype(jnp.bfloat16)
    ln2_bias = noise(splits[17], (D,), 0.5, 3.0, ((0, 32),))
    return dict(tokens=tokens, cotangent=cotangent, passage_lengths=passage_lengths, passage_counts=passage_counts, pad_counts=pad_counts, w_qkv=w_qkv, b_query=b_query, b_value=b_value, w_out=w_out, b_out=b_out, ln1_gain=ln1_gain, ln1_bias=ln1_bias, w_in=w_in, b_in=b_in, w_down=w_down, b_down=b_down, ln2_gain=ln2_gain, ln2_bias=ln2_bias)


@jax.custom_vjp
def low(v):
    return lax.optimization_barrier(v.astype(jnp.bfloat16)).astype(jnp.float32)

@jax.custom_vjp
def low_back(v):
    return v

def low_keep(v):
    return (low(v), None)

def low_pass(kept, grad):
    return (grad,)

def back_keep(v):
    return (v, None)

def back_low(kept, grad):
    return (low(grad),)
low.defvjp(low_keep, low_pass)
low_back.defvjp(back_keep, back_low)
norm_eps = 1e-12
neg_large = -1000000000.0
highest = lax.Precision.HIGHEST

def passage_ids(lengths, counts, pads, seq_len):
    slots = jnp.arange(lengths.shape[1], dtype=jnp.int32)
    inner = slots[None, :] < counts[:, None] - 1
    bounds = jnp.cumsum(jnp.where(inner, lengths, 0), axis=1)
    bounds = jnp.where(inner, bounds, (seq_len - pads)[:, None])
    places = jnp.arange(seq_len, dtype=jnp.int32)
    return lax.optimization_barrier(jnp.sum((places[None, :, None] >= bounds[:, None, :]).astype(jnp.int32), axis=2))

def normalize(v, gain, shift):
    centered = v - lax.optimization_barrier(jnp.mean(v, axis=-1, keepdims=True))
    inverse = lax.rsqrt(lax.optimization_barrier(jnp.mean(centered * centered, axis=-1, keepdims=True)) + norm_eps)
    return centered * inverse * gain + shift

def layer(x, same, w_qkv, b_query, b_value, w_out, b_out, ln1_gain, ln1_bias, w_in, b_in, w_down, b_down, ln2_gain, ln2_bias):
    batch, length, width = x.shape
    heads = width // HD
    x_low = low(x)
    joined_bias = jnp.concatenate([b_query, jnp.zeros_like(b_query), b_value])
    joined = jnp.einsum('bld,de->ble', x_low, w_qkv, precision=highest) + joined_bias
    joined = low(low_back(joined))
    query = joined[:, :, :width].reshape(batch, length, heads, HD)
    keys_all = joined[:, :, width:2 * width].reshape(batch, length, heads, HD)
    values = joined[:, :, 2 * width:].reshape(batch, length, heads, HD)
    scores = jnp.einsum('bqhe,bkhe->bhqk', query, keys_all, precision=highest) * (1.0 / math.sqrt(HD))
    scores = jnp.where(same[:, None, :, :], scores, neg_large)
    scores = low_back(scores)
    probs = low(jax.nn.softmax(scores, axis=-1))
    context = jnp.einsum('bhqk,bkhe->bqhe', probs, values, precision=highest).reshape(batch, length, width)
    context = low(low_back(context))
    branch = low_back(jnp.einsum('bld,de->ble', context, w_out, precision=highest) + b_out)
    y = normalize(x + branch, ln1_gain, ln1_bias)
    y_low = low(y)
    hidden_pre = low_back(jnp.einsum('bld,df->blf', y_low, w_in, precision=highest) + b_in)
    hidden = low(jax.nn.gelu(hidden_pre, approximate=False))
    ffn_out = low_back(jnp.einsum('blf,fd->bld', hidden, w_down, precision=highest) + b_down)
    return normalize(y + ffn_out, ln2_gain, ln2_bias)

def reference(tokens, cotangent, passage_lengths, passage_counts, pad_counts, w_qkv, b_query, b_value, w_out, b_out, ln1_gain, ln1_bias, w_in, b_in, w_down, b_down, ln2_gain, ln2_bias):
    weights = tuple((w.astype(jnp.float32) for w in (w_qkv, b_query, b_value, w_out, b_out, ln1_gain, ln1_bias, w_in, b_in, w_down, b_down, ln2_gain, ln2_bias)))
    ids = passage_ids(passage_lengths, passage_counts, pad_counts, SEQ_LEN)
    group = 8
    blocks = SEQS // group
    inputs = tokens.astype(jnp.float32).reshape(blocks, group, SEQ_LEN, D)
    grads_in = cotangent.astype(jnp.float32).reshape(blocks, group, SEQ_LEN, D)
    id_blocks = ids.reshape(blocks, group, SEQ_LEN)

    def step(carry, item):
        x_block, grad_block, id_block = item
        same = id_block[:, :, None] == id_block[:, None, :]

        def run(x_value, *weight_values):
            return layer(x_value, same, *weight_values)
        result, pull = jax.vjp(run, x_block, *weights)
        grads = pull(grad_block)
        carry = tuple((total + part for total, part in zip(carry, grads[1:])))
        return (carry, (result.astype(jnp.bfloat16), grads[0].astype(jnp.bfloat16)))
    init = tuple((jnp.zeros(w.shape, jnp.float32) for w in weights))
    totals, (results, token_grads) = lax.scan(step, init, (inputs, grads_in, id_blocks))
    return (results.reshape(TOKENS, D), token_grads.reshape(TOKENS, D), totals[0], totals[1], totals[2], totals[3], totals[4], totals[5], totals[6], totals[7], totals[8], totals[9], totals[10], totals[11], totals[12])
```

```python
import functools
import math

import jax
import jax.numpy as jnp
from jax import lax
from jax.experimental import pallas as pl
from jax.experimental.pallas import tpu as pltpu
from jax.sharding import PartitionSpec as P

HD = 64
SEQ_LEN = 512


norm_eps = 1e-12
neg_large = -1000000000.0


def passage_ids(lengths, counts, pads, seq_len):
    slots = jnp.arange(lengths.shape[1], dtype=jnp.int32)
    inner = slots[None, :] < counts[:, None] - 1
    bounds = jnp.cumsum(jnp.where(inner, lengths, 0), axis=1)
    bounds = jnp.where(inner, bounds, (seq_len - pads)[:, None])
    places = jnp.arange(seq_len, dtype=jnp.int32)
    return jnp.sum((places[None, :, None] >= bounds[:, None, :]).astype(jnp.int32), axis=2)


def normalize(value, gain, shift):
    centered = value - jnp.mean(value, axis=-1, keepdims=True)
    inverse = lax.rsqrt(jnp.mean(centered * centered, axis=-1, keepdims=True) + norm_eps)
    unit = centered * inverse
    return (unit * gain + shift, unit, inverse)


def normalize_back(grad_out, gain, unit, inverse):
    grad_unit = grad_out * gain
    return inverse * (
        grad_unit
        - jnp.mean(grad_unit, axis=-1, keepdims=True)
        - unit * jnp.mean(grad_unit * unit, axis=-1, keepdims=True)
    )


def gelu_slope(value):
    normal_cdf = 0.5 * (1.0 + lax.erf(value * (1.0 / math.sqrt(2.0))))
    return normal_cdf + value * jnp.exp(-0.5 * value * value) * (1.0 / math.sqrt(2.0 * math.pi))


def matmul(left, right):
    return jnp.dot(left, right, preferred_element_type=jnp.float32)


def matmul_left_t(left, right):
    return lax.dot_general(
        left, right, (((0,), (0,)), ((), ())), preferred_element_type=jnp.float32
    )


def matmul_right_t(left, right):
    return lax.dot_general(
        left, right, (((1,), (1,)), ((), ())), preferred_element_type=jnp.float32
    )


def head_slices(joined_seq, start, group, width):
    length = joined_seq.shape[0]
    column = start * HD
    span = group * HD
    query = joined_seq[:, column : column + span].reshape(length, group, HD)
    keys_part = joined_seq[:, width + column : width + column + span].reshape(length, group, HD)
    values = joined_seq[:, 2 * width + column : 2 * width + column + span].reshape(
        length, group, HD
    )
    return (query, keys_part, values)


def masked_scores(query, keys_part, same):
    scores = jnp.einsum("qhe,khe->hqk", query, keys_part, preferred_element_type=jnp.float32) * (
        1.0 / math.sqrt(HD)
    )
    return jnp.where(same[None, :, :], scores, neg_large)


def attend_forward(joined_seq, id_seq, width):
    heads = width // HD
    group = math.gcd(heads, 4)
    same = id_seq[:, None] == id_seq[None, :]
    length = joined_seq.shape[0]
    outputs = []
    totals = []
    for start in range(0, heads, group):
        query, keys_part, values = head_slices(joined_seq, start, group, width)
        scores = masked_scores(query, keys_part, same)
        top = jnp.max(scores, axis=2, keepdims=True)
        expo = jnp.exp(scores - top)
        total = jnp.sum(expo, axis=2, keepdims=True)
        probs = (expo / total).astype(jnp.bfloat16)
        mixed = jnp.einsum("hqk,khe->qhe", probs, values, preferred_element_type=jnp.float32)
        outputs.append(mixed.reshape(length, group * HD))
        totals.append((top + jnp.log(total))[:, :, 0])
    return (jnp.concatenate(outputs, axis=1).astype(jnp.bfloat16), jnp.concatenate(totals, axis=0))


def attend_back(joined_seq, grad_seq, log_seq, id_seq, width):
    heads = width // HD
    group = math.gcd(heads, 4)
    same = id_seq[:, None] == id_seq[None, :]
    length = joined_seq.shape[0]
    grad_queries = []
    grad_keys = []
    grad_values = []
    for start in range(0, heads, group):
        query, keys_part, values = head_slices(joined_seq, start, group, width)
        scores = masked_scores(query, keys_part, same)
        probs_full = jnp.exp(scores - log_seq[start : start + group][:, :, None])
        probs = probs_full.astype(jnp.bfloat16)
        grad_mixed = grad_seq[:, start * HD : (start + group) * HD].reshape(length, group, HD)
        grad_probs = jnp.einsum(
            "qhe,khe->hqk", grad_mixed, values, preferred_element_type=jnp.float32
        )
        grad_values.append(
            jnp.einsum(
                "hqk,qhe->khe", probs, grad_mixed, preferred_element_type=jnp.float32
            ).reshape(length, group * HD)
        )
        grad_scores = (
            probs_full * (grad_probs - jnp.sum(grad_probs * probs_full, axis=2, keepdims=True))
        ).astype(jnp.bfloat16)
        grad_queries.append(
            (
                jnp.einsum(
                    "hqk,khe->qhe", grad_scores, keys_part, preferred_element_type=jnp.float32
                )
                * (1.0 / math.sqrt(HD))
            ).reshape(length, group * HD)
        )
        grad_keys.append(
            (
                jnp.einsum("hqk,qhe->khe", grad_scores, query, preferred_element_type=jnp.float32)
                * (1.0 / math.sqrt(HD))
            ).reshape(length, group * HD)
        )
    return jnp.concatenate(grad_queries + grad_keys + grad_values, axis=1).astype(jnp.bfloat16)


MESH = pl.DeviceIdType.MESH
bf16 = jnp.bfloat16
f32 = jnp.float32
VEC_LANES = 768
VEC_ROWS = 16


def cut(start, size, shares):
    out = []
    for share in shares:
        out.append((start, share))
        start += share
    return out


def chunk(tensor, rows, first, cols):
    if rows >= 96:
        step = rows // 6
        parts = cut(0, rows, (step, 2 * step, 2 * step, step))
        box = lambda lo, hi: (slice(parts[lo][0], parts[hi][0] + parts[hi][1]), slice(first, first + cols))
    else:
        step = cols // 6 // 128 * 128
        parts = cut(first, cols, (step, cols // 2 - step, cols // 2 - step, step))
        box = lambda lo, hi: (slice(0, rows), slice(parts[lo][0], parts[hi][0] + parts[hi][1]))
    return dict(
        tensor=tensor,
        rows=rows,
        first=first,
        cols=cols,
        c1=box(0, 0), a1=box(1, 1), a2=box(2, 2), c2=box(3, 3),
        a=box(1, 2), left=box(0, 1), right=box(2, 3), all=box(0, 3),
    )


def shape_of(part):
    return (part[0].stop - part[0].start, part[1].stop - part[1].start)


def at(part):
    return (pl.ds(part[0].start, part[0].stop - part[0].start), pl.ds(part[1].start, part[1].stop - part[1].start))


class Place:
    def __init__(self):
        w = lax.axis_index("wide")
        self.z = lax.axis_index("narrow")
        self.w = w
        self.c = lax.rem(w, 2)
        self.x = lax.rem(lax.div(w, 2), 2)
        self.y = lax.div(w, 4)

    def to(self, which):
        if which == "c":
            return (self.w + 1 - 2 * self.c, self.z)
        if which == "x":
            return (self.w + 2 - 4 * self.x, self.z)
        if which == "y":
            return (self.w + 4 - 8 * self.y, self.z)
        return (self.w, lax.rem(self.z + which, 4))


def greet(me):
    barrier = pltpu.get_barrier_semaphore()
    peers = ("c", "x", "y", 1, 2, 3)
    for which in peers:
        pl.semaphore_signal(barrier, inc=1, device_id=me.to(which), device_id_type=MESH)
    pl.semaphore_wait(barrier, len(peers))


class Gather:
    def __init__(self, me, piece, own, full, sems):
        self.me, self.piece, self.own, self.full, self.sems = me, piece, own, full, sems
        self.sent = []
        self.due = {}

    def send(self, stage, slot, src, dst, which):
        copy = pltpu.make_async_remote_copy(
            src_ref=src, dst_ref=dst, send_sem=self.sems.at[0, slot], recv_sem=self.sems.at[1, slot],
            device_id=self.me.to(which), device_id_type=MESH,
        )
        copy.start()
        self.sent.append(copy)
        self.due.setdefault(stage, []).append(copy)

    def block(self, part, y=None, x=None, z=None):
        me, full = self.me, self.full
        pick = (me.y if y is None else y, me.x if x is None else x, me.c, me.z if z is None else z)
        return full.at[(*pick, *at(part))]

    def run(self, stage):
        p, me = self.piece, self.me
        every = pl.ds(0, 2)
        line = pl.ds(0, 4)
        for copy in self.due.get(stage - 1, ()):
            copy.wait_recv()
        if stage == 1:
            for k in (1, 2, 3):
                self.send(1, k - 1, self.own.at[at(p["a"])], self.block(p["a"]), k)
            self.send(1, 3, self.own.at[at(p["c1"])], self.block(p["c1"]), "x")
            self.send(1, 4, self.own.at[at(p["c2"])], self.block(p["c2"]), "y")
        elif stage == 2:
            src = self.block(p["a1"], z=line)
            self.send(2, 5, src, src, "x")
            src = self.block(p["a2"], z=line)
            self.send(2, 6, src, src, "y")
            for k in (1, 2, 3):
                src = self.block(p["c1"], x=every)
                self.send(2, 6 + k, src, src, k)
                src = self.block(p["c2"], y=every)
                self.send(2, 9 + k, src, src, k)
        elif stage == 3:
            src = self.block(p["left"], x=every, z=line)
            self.send(3, 13, src, src, "y")
            src = self.block(p["right"], y=every, z=line)
            self.send(3, 14, src, src, "x")
        elif stage == 4:
            src = self.block(p["all"], y=every, x=every, z=line)
            self.send(4, 15, src, src, "c")

    def finish(self):
        for copy in self.sent:
            copy.wait_send()


class Scatter:
    def __init__(self, me, piece, partial, out, bufs, sems):
        self.me, self.piece, self.partial, self.out, self.sems = me, piece, partial, out, sems
        self.sib, self.inl, self.inr, self.ina1, self.ina2, self.inc1, self.inc2, self.lasta, self.lastc1, self.lastc2 = bufs
        self.sent = []
        self.due = {}

    send = Gather.send

    def buffers(piece):
        rows = lambda part: shape_of(piece[part])
        return (
            (2, 2, 4, *rows("all")), (2, 4, *rows("left")), (2, 4, *rows("right")),
            (4, *rows("a1")), (4, *rows("a2")), (3, 2, *rows("c1")), (3, 2, *rows("c2")),
            (3, *rows("a")), rows("c1"), rows("c2"),
        )

    def inner(self, part):
        box, whole = self.piece[part], self.piece["all"]
        rows, cols = shape_of(box)
        return (pl.ds(box[0].start - whole[0].start, rows), pl.ds(box[1].start - whole[1].start, cols))

    def run(self, stage):
        p, me = self.piece, self.me
        every, line = pl.ds(0, 2), pl.ds(0, 4)
        up = lambda v: v.astype(f32)
        left, right, a, a1, a2, c1, c2 = (self.inner(k) for k in ("left", "right", "a", "a1", "a2", "c1", "c2"))
        for copy in self.due.get(stage - 1, ()):
            copy.wait_recv()
        ox, oy = 1 - me.x, 1 - me.y
        peers = [lax.rem(me.z + k, 4) for k in (1, 2, 3)]
        if stage == 1:
            self.send(1, 0, self.partial.at[:, :, 1 - me.c, :, *at(p["all"])], self.sib, "c")
        elif stage == 2:
            for y in (0, 1):
                for x in (0, 1):
                    mine = self.partial[y, x, me.c, :, *at(p["all"])]
                    self.sib[y, x] = (up(mine) + up(self.sib[y, x])).astype(bf16)
            self.send(2, 1, self.sib.at[oy, every, line, *left], self.inl, "y")
            self.send(2, 2, self.sib.at[every, ox, line, *right], self.inr, "x")
        elif stage == 3:
            for k in (0, 1):
                self.inl[k] = (up(self.inl[k]) + up(self.sib[me.y, k, :, *left])).astype(bf16)
                self.inr[k] = (up(self.inr[k]) + up(self.sib[k, me.x, :, *right])).astype(bf16)
            in_left = lambda part: (self.inner(part)[0], self.inner(part)[1])
            self.la1, self.lc1 = self.sub("left", "a1"), self.sub("left", "c1")
            self.ra2, self.rc2 = self.sub("right", "a2"), self.sub("right", "c2")
            self.send(3, 3, self.inl.at[ox, line, *self.la1], self.ina1, "x")
            self.send(3, 4, self.inr.at[oy, line, *self.ra2], self.ina2, "y")
            for k, z in zip((1, 2, 3), peers):
                self.send(3, 4 + k, self.inl.at[every, z, *self.lc1], self.inc1.at[k - 1], k)
                self.send(3, 7 + k, self.inr.at[every, z, *self.rc2], self.inc2.at[k - 1], k)
        elif stage == 4:
            self.ina1[...] = (up(self.ina1[...]) + up(self.inl[me.x, :, *self.la1])).astype(bf16)
            self.ina2[...] = (up(self.ina2[...]) + up(self.inr[me.y, :, *self.ra2])).astype(bf16)
            total = up(self.inc1[0]) + up(self.inc1[1]) + up(self.inc1[2]) + up(self.inl[:, me.z, *self.lc1])
            self.inc1[0] = total.astype(bf16)
            total = up(self.inc2[0]) + up(self.inc2[1]) + up(self.inc2[2]) + up(self.inr[:, me.z, *self.rc2])
            self.inc2[0] = total.astype(bf16)
            self.aa1, self.aa2 = self.sub("a", "a1"), self.sub("a", "a2")
            for k, z in zip((1, 2, 3), peers):
                self.send(4, 10 + k, self.ina1.at[z], self.lasta.at[k - 1, *self.aa1], k)
                self.send(4, 13 + k, self.ina2.at[z], self.lasta.at[k - 1, *self.aa2], k)
            self.send(4, 17, self.inc1.at[0, ox], self.lastc1, "x")
            self.send(4, 18, self.inc2.at[0, oy], self.lastc2, "y")
        elif stage == 5:
            for sub, got, part in ((self.aa1, self.ina1, "a1"), (self.aa2, self.ina2, "a2")):
                total = up(got[me.z])
                for k in (0, 1, 2):
                    total = total + up(self.lasta[k, *sub])
                self.out[at(p[part])] = total
            self.out[at(p["c1"])] = up(self.inc1[0, me.x]) + up(self.lastc1[...])
            self.out[at(p["c2"])] = up(self.inc2[0, me.y]) + up(self.lastc2[...])

    def sub(self, outer, part):
        box, whole = self.piece[part], self.piece[outer]
        rows, cols = shape_of(box)
        return (pl.ds(box[0].start - whole[0].start, rows), pl.ds(box[1].start - whole[1].start, cols))

    finish = Gather.finish


class SumVectors:
    def __init__(self, me, value, got, hold, out, sems):
        self.me, self.value, self.got, self.hold, self.out, self.sems = me, value, got, hold, out, sems
        self.sent = []
        self.due = {}

    send = Gather.send

    def run(self, stage):
        for copy in self.due.get(stage - 1, ()):
            copy.wait_recv()
        if stage == 1:
            self.send(1, 0, self.value, self.got.at[0], "c")
        elif stage == 2:
            self.hold[0] = self.value[...] + self.got[0]
            self.send(2, 1, self.hold.at[0], self.got.at[1], "x")
        elif stage == 3:
            self.hold[1] = self.hold[0] + self.got[1]
            self.send(3, 2, self.hold.at[1], self.got.at[2], "y")
        elif stage == 4:
            self.hold[2] = self.hold[1] + self.got[2]
            for k in (1, 2, 3):
                self.send(4, 2 + k, self.hold.at[2], self.got.at[2 + k], k)
        elif stage == 5:
            self.out[...] = (self.hold[2] + self.got[3]) + (self.got[4] + self.got[5])

    finish = Gather.finish


def rotate(items, stages, apart):
    for slot in range(len(items) + (stages - 1) * apart):
        for stage in range(stages, 0, -1):
            at_item = slot - (stage - 1) * apart
            if 0 <= at_item < len(items):
                items[at_item].run(stage)
    for item in items:
        item.finish()


def gather_chunks(rows, big_rows, width, wide):
    chunks = [chunk(4, 8, 0, VEC_LANES)]
    chunks += [chunk(0, rows, k * width, width) for k in range(3)]
    chunks += [chunk(1, rows, 0, width)]
    chunks += [chunk(2, rows, k * width, width) for k in range(wide // width)]
    chunks += [chunk(3, big_rows, k * 256, 256) for k in range(width // 256)]
    return chunks


def scatter_chunks(rows, big_rows, width, wide):
    chunks = [chunk(3, big_rows, k * 256, 256) for k in range(width // 256)]
    chunks += [chunk(2, rows, k * width, width) for k in range(wide // width)]
    chunks += [chunk(1, rows, 0, width)]
    chunks += [chunk(0, rows, k * width, width) for k in range(3)]
    return chunks


def gather_kernel(chunks, *refs):
    owns, fulls, sems = refs[:5], refs[5:10], refs[10]
    me = Place()
    greet(me)
    for own, full in zip(owns, fulls):
        full[me.y, me.x, me.c, me.z] = own[...]
    items = [Gather(me, p, owns[p["tensor"]], fulls[p["tensor"]], sems.at[n]) for n, p in enumerate(chunks)]
    rotate(items, 5, 1)


def gather_all(owns, chunks):
    grid = (2, 2, 2, 4)
    vmem = pl.BlockSpec(memory_space=pltpu.VMEM)
    return pl.pallas_call(
        functools.partial(gather_kernel, chunks),
        out_shape=[jax.ShapeDtypeStruct(grid + own.shape, own.dtype) for own in owns],
        in_specs=[vmem] * 5,
        out_specs=[vmem] * 5,
        scratch_shapes=[pltpu.SemaphoreType.DMA((len(chunks), 2, 16))],
        compiler_params=pltpu.CompilerParams(collective_id=0, has_side_effects=True, vmem_limit_bytes=56 * 2**20),
        name="gather_weights",
    )(*owns)


def scatter_kernel(chunks, *refs):
    partials, vec, outs, vec_out = refs[:4], refs[4], refs[5:9], refs[9]
    sems, vec_sems, got, hold = refs[10:14]
    rest = refs[14:]
    me = Place()
    greet(me)
    items = []
    for n, p in enumerate(chunks):
        bufs = rest[10 * n : 10 * n + 10]
        items.append(Scatter(me, p, partials[p["tensor"]], outs[p["tensor"]], bufs, sems.at[n]))
    items.insert(len(items) - 1, SumVectors(me, vec, got, hold, vec_out, vec_sems))
    rotate(items, 5, 1)


def scatter_all(partials, vec, chunks):
    vmem = pl.BlockSpec(memory_space=pltpu.VMEM)
    scratch = [
        pltpu.SemaphoreType.DMA((len(chunks), 2, 19)),
        pltpu.SemaphoreType.DMA((2, 6)),
        pltpu.VMEM((6, *vec.shape), f32),
        pltpu.VMEM((3, *vec.shape), f32),
    ]
    for p in chunks:
        scratch += [pltpu.VMEM(shape, bf16) for shape in Scatter.buffers(p)]
    return pl.pallas_call(
        functools.partial(scatter_kernel, chunks),
        out_shape=[jax.ShapeDtypeStruct(p.shape[4:], f32) for p in partials] + [jax.ShapeDtypeStruct(vec.shape, f32)],
        in_specs=[vmem] * 5,
        out_specs=[vmem] * 5,
        scratch_shapes=scratch,
        compiler_params=pltpu.CompilerParams(collective_id=1, has_side_effects=True, vmem_limit_bytes=56 * 2**20),
        name="scatter_grads",
    )(*partials, vec)


def direct(
    tokens,
    cotangent,
    passage_lengths,
    passage_counts,
    pad_counts,
    w_qkv,
    b_query,
    b_value,
    w_out,
    b_out,
    ln1_gain,
    ln1_bias,
    w_in,
    b_in,
    w_down,
    b_down,
    ln2_gain,
    ln2_bias,
):
    width = tokens.shape[1]
    rows_here = passage_counts.shape[0]
    positions = tokens.shape[0]
    packed = jnp.concatenate([b_query, b_value, b_out, ln1_gain, ln1_bias, b_down, ln2_gain, ln2_bias, b_in])
    packed = jnp.pad(packed[None, :], ((0, 7), (0, VEC_LANES - packed.shape[0])))
    rows, big_rows, wide = w_qkv.shape[0], w_down.shape[0], w_in.shape[1]
    chunks = gather_chunks(rows, big_rows, width, wide)
    full_qkv, full_out, full_in, full_down, full_vec = gather_all((w_qkv, w_out, w_in, w_down, packed), chunks)
    full_qkv = full_qkv.reshape(width, 3 * width)
    full_out = full_out.reshape(width, width)
    full_in = full_in.reshape(width, wide)
    full_down = full_down.reshape(wide, width)
    full_vec = full_vec.reshape(32, 8, VEC_LANES)[:, 0, :]
    full_bq, full_bv, full_bout, full_g1, full_c1, full_bdown, full_g2, full_c2 = (
        full_vec[:, k * rows : (k + 1) * rows].reshape(width) for k in range(8)
    )
    full_bin = full_vec[:, 8 * rows : 8 * rows + big_rows].reshape(wide)
    ids = passage_ids(passage_lengths, passage_counts, pad_counts, SEQ_LEN)
    joined_bias = jnp.concatenate([full_bq, jnp.zeros_like(full_bq), full_bv]).astype(jnp.float32)
    joined = (matmul(tokens, full_qkv) + joined_bias).astype(jnp.bfloat16)
    joined_rows = joined.reshape(rows_here, SEQ_LEN, 3 * width)
    context, log_total = lax.map(
        lambda item: attend_forward(item[0], item[1], width), (joined_rows, ids)
    )
    context = context.reshape(positions, width)
    x_value = tokens.astype(jnp.float32)
    mid = x_value + matmul(context, full_out) + full_bout.astype(jnp.float32)
    y_value, unit_one, inverse_one = normalize(
        mid, full_g1.astype(jnp.float32), full_c1.astype(jnp.float32)
    )
    y_low = y_value.astype(jnp.bfloat16)
    hidden_pre = matmul(y_low, full_in) + full_bin.astype(jnp.float32)
    hidden = jax.nn.gelu(hidden_pre, approximate=False).astype(jnp.bfloat16)
    z_value = y_value + matmul(hidden, full_down) + full_bdown.astype(jnp.float32)
    result, unit_two, inverse_two = normalize(
        z_value, full_g2.astype(jnp.float32), full_c2.astype(jnp.float32)
    )
    activations = result.astype(jnp.bfloat16)
    back_qkv = full_qkv
    back_out = full_out
    back_g1 = full_g1.astype(jnp.float32)
    back_in = full_in
    back_down = full_down
    back_g2 = full_g2.astype(jnp.float32)
    grad_top = cotangent.astype(jnp.float32)
    ln2_gain_grad = jnp.sum(grad_top * unit_two, axis=0)
    ln2_bias_grad = jnp.sum(grad_top, axis=0)
    grad_z = normalize_back(grad_top, back_g2, unit_two, inverse_two)
    grad_ffn = grad_z.astype(jnp.bfloat16)
    w_down_grad = matmul_left_t(hidden, grad_ffn)
    b_down_grad = jnp.sum(grad_ffn, axis=0, dtype=jnp.float32)
    grad_pre = (matmul_right_t(grad_ffn, back_down) * gelu_slope(hidden_pre)).astype(jnp.bfloat16)
    w_in_grad = matmul_left_t(y_low, grad_pre)
    b_in_grad = jnp.sum(grad_pre, axis=0, dtype=jnp.float32)
    grad_y = grad_z + matmul_right_t(grad_pre, back_in)
    ln1_gain_grad = jnp.sum(grad_y * unit_one, axis=0)
    ln1_bias_grad = jnp.sum(grad_y, axis=0)
    grad_mid = normalize_back(grad_y, back_g1, unit_one, inverse_one)
    grad_branch = grad_mid.astype(jnp.bfloat16)
    w_out_grad = matmul_left_t(context, grad_branch)
    b_out_grad = jnp.sum(grad_branch, axis=0, dtype=jnp.float32)
    grad_context = matmul_right_t(grad_branch, back_out).astype(jnp.bfloat16)
    grad_joined = lax.map(
        lambda item: attend_back(item[0], item[1], item[2], item[3], width),
        (joined_rows, grad_context.reshape(rows_here, SEQ_LEN, width), log_total, ids),
    )
    grad_joined = grad_joined.reshape(positions, 3 * width)
    w_qkv_grad = matmul_left_t(tokens, grad_joined)
    column_sums = jnp.sum(grad_joined, axis=0, dtype=jnp.float32)
    b_query_grad = column_sums[:width]
    b_value_grad = column_sums[2 * width :]
    token_grad = (grad_mid + matmul_right_t(grad_joined, back_qkv)).astype(jnp.bfloat16)
    grid = (2, 2, 2, 4)
    partials = [
        w_qkv_grad.astype(bf16).reshape(*grid, rows, 3 * width),
        w_out_grad.astype(bf16).reshape(*grid, rows, width),
        w_in_grad.astype(bf16).reshape(*grid, rows, wide),
        w_down_grad.astype(bf16).reshape(*grid, big_rows, width),
    ]
    vec = jnp.concatenate(
        [b_query_grad, b_value_grad, b_out_grad, ln1_gain_grad, ln1_bias_grad, b_down_grad, ln2_gain_grad, ln2_bias_grad, b_in_grad]
    ).reshape(8 + wide // width, width)
    vec = jnp.pad(vec, ((0, VEC_ROWS - vec.shape[0]), (0, 0)))
    chunks = scatter_chunks(rows, big_rows, width, wide)
    own_qkv, own_out, own_in, own_down, vec = scatter_all(partials, vec, chunks)
    place = lax.axis_index(("wide", "narrow"))
    small = lax.dynamic_slice(vec[:8], (0, place * rows), (8, rows))
    own_bin = lax.dynamic_slice(vec[8 : 8 + wide // width].reshape(wide), (place * big_rows,), (big_rows,))
    return (
        activations, token_grad, own_qkv, small[0], small[1], own_out, small[2], small[3], small[4],
        own_in, own_bin, own_down, small[5], small[6], small[7],
    )


def on_device(
    tokens,
    cotangent,
    passage_lengths,
    passage_counts,
    pad_counts,
    w_qkv,
    b_query,
    b_value,
    w_out,
    b_out,
    ln1_gain,
    ln1_bias,
    w_in,
    b_in,
    w_down,
    b_down,
    ln2_gain,
    ln2_bias,
):
    width = tokens.shape[1]
    rows_here = passage_counts.shape[0]
    positions = tokens.shape[0]
    gathered = (
        lax.all_gather(w_qkv, ("wide", "narrow"), axis=0, tiled=True),
        lax.all_gather(b_query, ("wide", "narrow"), axis=0, tiled=True),
        lax.all_gather(b_value, ("wide", "narrow"), axis=0, tiled=True),
        lax.all_gather(w_out, ("wide", "narrow"), axis=0, tiled=True),
        lax.all_gather(b_out, ("wide", "narrow"), axis=0, tiled=True),
        lax.all_gather(ln1_gain, ("wide", "narrow"), axis=0, tiled=True),
        lax.all_gather(ln1_bias, ("wide", "narrow"), axis=0, tiled=True),
        lax.all_gather(w_in, ("wide", "narrow"), axis=0, tiled=True),
        lax.all_gather(b_in, ("wide", "narrow"), axis=0, tiled=True),
        lax.all_gather(w_down, ("wide", "narrow"), axis=0, tiled=True),
        lax.all_gather(b_down, ("wide", "narrow"), axis=0, tiled=True),
        lax.all_gather(ln2_gain, ("wide", "narrow"), axis=0, tiled=True),
        lax.all_gather(ln2_bias, ("wide", "narrow"), axis=0, tiled=True),
    )
    (
        full_qkv,
        full_bq,
        full_bv,
        full_out,
        full_bout,
        full_g1,
        full_c1,
        full_in,
        full_bin,
        full_down,
        full_bdown,
        full_g2,
        full_c2,
    ) = gathered
    ids = passage_ids(passage_lengths, passage_counts, pad_counts, SEQ_LEN)
    joined_bias = jnp.concatenate([full_bq, jnp.zeros_like(full_bq), full_bv]).astype(jnp.float32)
    joined = (matmul(tokens, full_qkv) + joined_bias).astype(jnp.bfloat16)
    joined_rows = joined.reshape(rows_here, SEQ_LEN, 3 * width)
    context, log_total = lax.map(
        lambda item: attend_forward(item[0], item[1], width), (joined_rows, ids)
    )
    context = context.reshape(positions, width)
    x_value = tokens.astype(jnp.float32)
    mid = x_value + matmul(context, full_out) + full_bout.astype(jnp.float32)
    y_value, unit_one, inverse_one = normalize(
        mid, full_g1.astype(jnp.float32), full_c1.astype(jnp.float32)
    )
    y_low = y_value.astype(jnp.bfloat16)
    hidden_pre = matmul(y_low, full_in) + full_bin.astype(jnp.float32)
    hidden = jax.nn.gelu(hidden_pre, approximate=False).astype(jnp.bfloat16)
    z_value = y_value + matmul(hidden, full_down) + full_bdown.astype(jnp.float32)
    result, unit_two, inverse_two = normalize(
        z_value, full_g2.astype(jnp.float32), full_c2.astype(jnp.float32)
    )
    activations = result.astype(jnp.bfloat16)
    again = (
        lax.all_gather(w_qkv, ("wide", "narrow"), axis=0, tiled=True),
        lax.all_gather(b_query, ("wide", "narrow"), axis=0, tiled=True),
        lax.all_gather(b_value, ("wide", "narrow"), axis=0, tiled=True),
        lax.all_gather(w_out, ("wide", "narrow"), axis=0, tiled=True),
        lax.all_gather(b_out, ("wide", "narrow"), axis=0, tiled=True),
        lax.all_gather(ln1_gain, ("wide", "narrow"), axis=0, tiled=True),
        lax.all_gather(ln1_bias, ("wide", "narrow"), axis=0, tiled=True),
        lax.all_gather(w_in, ("wide", "narrow"), axis=0, tiled=True),
        lax.all_gather(b_in, ("wide", "narrow"), axis=0, tiled=True),
        lax.all_gather(w_down, ("wide", "narrow"), axis=0, tiled=True),
        lax.all_gather(b_down, ("wide", "narrow"), axis=0, tiled=True),
        lax.all_gather(ln2_gain, ("wide", "narrow"), axis=0, tiled=True),
        lax.all_gather(ln2_bias, ("wide", "narrow"), axis=0, tiled=True),
    )
    back_qkv = again[0]
    back_out = again[3]
    back_g1 = again[5].astype(jnp.float32)
    back_in = again[7]
    back_down = again[9]
    back_g2 = again[11].astype(jnp.float32)
    grad_top = cotangent.astype(jnp.float32)
    ln2_gain_grad = jnp.sum(grad_top * unit_two, axis=0)
    ln2_bias_grad = jnp.sum(grad_top, axis=0)
    grad_z = normalize_back(grad_top, back_g2, unit_two, inverse_two)
    grad_ffn = grad_z.astype(jnp.bfloat16)
    w_down_grad = matmul_left_t(hidden, grad_ffn)
    b_down_grad = jnp.sum(grad_ffn, axis=0, dtype=jnp.float32)
    grad_pre = (matmul_right_t(grad_ffn, back_down) * gelu_slope(hidden_pre)).astype(jnp.bfloat16)
    w_in_grad = matmul_left_t(y_low, grad_pre)
    b_in_grad = jnp.sum(grad_pre, axis=0, dtype=jnp.float32)
    grad_y = grad_z + matmul_right_t(grad_pre, back_in)
    ln1_gain_grad = jnp.sum(grad_y * unit_one, axis=0)
    ln1_bias_grad = jnp.sum(grad_y, axis=0)
    grad_mid = normalize_back(grad_y, back_g1, unit_one, inverse_one)
    grad_branch = grad_mid.astype(jnp.bfloat16)
    w_out_grad = matmul_left_t(context, grad_branch)
    b_out_grad = jnp.sum(grad_branch, axis=0, dtype=jnp.float32)
    grad_context = matmul_right_t(grad_branch, back_out).astype(jnp.bfloat16)
    grad_joined = lax.map(
        lambda item: attend_back(item[0], item[1], item[2], item[3], width),
        (joined_rows, grad_context.reshape(rows_here, SEQ_LEN, width), log_total, ids),
    )
    grad_joined = grad_joined.reshape(positions, 3 * width)
    w_qkv_grad = matmul_left_t(tokens, grad_joined)
    column_sums = jnp.sum(grad_joined, axis=0, dtype=jnp.float32)
    b_query_grad = column_sums[:width]
    b_value_grad = column_sums[2 * width :]
    token_grad = (grad_mid + matmul_right_t(grad_joined, back_qkv)).astype(jnp.bfloat16)
    owned = (
        lax.psum_scatter(w_qkv_grad, ("wide", "narrow"), scatter_dimension=0, tiled=True),
        lax.psum_scatter(b_query_grad, ("wide", "narrow"), scatter_dimension=0, tiled=True),
        lax.psum_scatter(b_value_grad, ("wide", "narrow"), scatter_dimension=0, tiled=True),
        lax.psum_scatter(w_out_grad, ("wide", "narrow"), scatter_dimension=0, tiled=True),
        lax.psum_scatter(b_out_grad, ("wide", "narrow"), scatter_dimension=0, tiled=True),
        lax.psum_scatter(ln1_gain_grad, ("wide", "narrow"), scatter_dimension=0, tiled=True),
        lax.psum_scatter(ln1_bias_grad, ("wide", "narrow"), scatter_dimension=0, tiled=True),
        lax.psum_scatter(w_in_grad, ("wide", "narrow"), scatter_dimension=0, tiled=True),
        lax.psum_scatter(b_in_grad, ("wide", "narrow"), scatter_dimension=0, tiled=True),
        lax.psum_scatter(w_down_grad, ("wide", "narrow"), scatter_dimension=0, tiled=True),
        lax.psum_scatter(b_down_grad, ("wide", "narrow"), scatter_dimension=0, tiled=True),
        lax.psum_scatter(ln2_gain_grad, ("wide", "narrow"), scatter_dimension=0, tiled=True),
        lax.psum_scatter(ln2_bias_grad, ("wide", "narrow"), scatter_dimension=0, tiled=True),
    )
    return (
        activations,
        token_grad,
        owned[0],
        owned[1],
        owned[2],
        owned[3],
        owned[4],
        owned[5],
        owned[6],
        owned[7],
        owned[8],
        owned[9],
        owned[10],
        owned[11],
        owned[12],
    )


def solution(mesh):
    placed = (
        P(("wide", "narrow"), None),
        P(("wide", "narrow"), None),
        P(("wide", "narrow"), None),
        P(("wide", "narrow")),
        P(("wide", "narrow")),
        P(("wide", "narrow"), None),
        P(("wide", "narrow")),
        P(("wide", "narrow")),
        P(("wide", "narrow"), None),
        P(("wide", "narrow")),
        P(("wide", "narrow")),
        P(("wide", "narrow")),
        P(("wide", "narrow"), None),
        P(("wide", "narrow")),
        P(("wide", "narrow"), None),
        P(("wide", "narrow")),
        P(("wide", "narrow")),
        P(("wide", "narrow")),
    )
    fits = (mesh.shape["wide"], mesh.shape["narrow"]) == (8, 4)
    return jax.shard_map(
        direct if fits else on_device,
        mesh=mesh,
        in_specs=placed,
        out_specs=(
            P(("wide", "narrow"), None),
            P(("wide", "narrow"), None),
            P(("wide", "narrow"), None),
            P(("wide", "narrow")),
            P(("wide", "narrow")),
            P(("wide", "narrow"), None),
            P(("wide", "narrow")),
            P(("wide", "narrow")),
            P(("wide", "narrow")),
            P(("wide", "narrow"), None),
            P(("wide", "narrow")),
            P(("wide", "narrow"), None),
            P(("wide", "narrow")),
            P(("wide", "narrow")),
            P(("wide", "narrow")),
        ),
        check_vma=False,
    )
```
